128 devices in a mesh: dp: 8 (over z_hi, y), tensor: 4 (over z_lo, core), replica: 4 (over x).
Axes of the slice: x: 4, y: 4, z: 4 (z_hi: 2, z_lo: 2; z = z_hi * 2 + z_lo), core: 2. Of those that a mesh axis runs over, the one named last changes fastest.
Arguments:
- queries: bfloat16 [8192, 8192], P(('dp', 'replica'), 'tensor'), may hold values from -8 to 8
- d_out: bfloat16 [8192, 8192], P(('dp', 'replica'), 'tensor'), may hold values from -48 to 48
- conv_keys: bfloat16 [8192, 1024], P(('dp', 'replica'), 'tensor'), may hold values from -12 to 12
- conv_values: bfloat16 [8192, 1024], P(('dp', 'replica'), 'tensor'), may hold values from -6 to 6
- segment_ids: int32 [32, 256], P(('dp', 'replica')), may hold values from 0 to 3, never falling along the last dimension, each value on 1 to 192 neighbouring positions
- master_keys: float32 [4096, 1024], P('dp', 'tensor'), may hold values from -8 to 8
- master_values: float32 [4096, 1024], P('dp', 'tensor'), may hold values from -6 to 6
- moment_keys: float32 [4096, 1024], P('dp', 'tensor'), may hold values from -3 to 3
- moment_values: float32 [4096, 1024], P('dp', 'tensor'), may hold values from -3 to 3
- second_keys: float32 [4096, 1024], P('dp', 'tensor'), may hold values from 0.01 to 1
- second_values: float32 [4096, 1024], P('dp', 'tensor'), may hold values from 0.01 to 1
Outputs:
- new_master_keys: float32 [4096, 1024], P('dp', 'tensor')
- new_master_values: float32 [4096, 1024], P('dp', 'tensor')
- new_moment_keys: float32 [4096, 1024], P('dp', 'tensor')
- new_moment_values: float32 [4096, 1024], P('dp', 'tensor')
- new_second_keys: float32 [4096, 1024], P('dp', 'tensor')
- new_second_values: float32 [4096, 1024], P('dp', 'tensor')
- served_keys: bfloat16 [4096, 1024], P(None, 'tensor')
- served_values: bfloat16 [4096, 1024], P(None, 'tensor')
- grad_keys: float32 [4096, 1024], P('dp', 'tensor')
- grad_values: float32 [4096, 1024], P('dp', 'tensor')
The draws below stay inside these ranges and needn't reach their ends.
Inputs may be any that keep to these rules, and one draw needn't show every extreme that they name: `segment_ids`: each row holds the conversation numbers of one device's 256 tokens.
All inputs are finite; a program needn't handle non-finite values.
Results may differ from the reference program's by a relative error of at most 0.0065.
Values may be sent and summed in bfloat16 or wider, within the bound.
No kernel may reach another device: no remote copies, remote signals or barrier semaphores. Data moves between devices by JAX's collectives and lax.ppermute only.
A program may use at most 256 MiB of HBM per device.

```python
import math
import jax
import jax.numpy as jnp
import numpy as np
from jax import lax

Q_HEADS = 64
KV_HEADS = 8
HEAD_DIM = 128
P_SIZE = 4096
TOK_DEV = 256
STEP = 20
TOKENS = 8192
N_DP = 8
N_REPLICA = 4


def draw_queries(key, part):
    drawn = jnp.clip(jax.random.normal(jax.random.fold_in(key, 11), (TOKENS, Q_HEADS * HEAD_DIM), jnp.float32), -6.0, 6.0)
    return drawn.astype(jnp.bfloat16)


def draw_master_keys(key, part):
    drawn = jnp.clip(jax.random.normal(jax.random.fold_in(key, 13), (P_SIZE, KV_HEADS * HEAD_DIM), jnp.float32), -6.0, 6.0)
    return drawn


def draw_master_values(key, part):
    columns = KV_HEADS * HEAD_DIM
    picks = jax.random.bernoulli(jax.random.fold_in(key, 21), 0.5, (columns,))
    column_sign = jnp.where(picks, 1.0, -1.0).astype(jnp.float32)
    column_size = jax.random.uniform(jax.random.fold_in(key, 23), (columns,), jnp.float32, 0.5, 1.5)
    noise = jnp.clip(jax.random.normal(jax.random.fold_in(key, 31), (P_SIZE, columns), jnp.float32), -4.5, 4.5)
    return (column_sign * column_size)[None, :] + noise


def level_of(rng, shape, shards, low, high):
    def one(position, blocks):
        draws = jax.random.uniform(jax.random.fold_in(jax.random.fold_in(rng, 6), position), (blocks,), jnp.float32, low / len(shards), high / len(shards))
        return jnp.repeat(jnp.exp(draws), shape[position] // blocks).reshape((-1,) + (1,) * (len(shape) - position - 1))

    level = one(*shards[0])
    for cut in shards[1:]:
        level = level * one(*cut)
    return level


def profile(amount, total, reach, slope):
    loads = [(1 << 20) // math.isqrt(grade ** slope) + 1 for grade in range(2, amount + 1)]
    spare, given = total - reach - (amount - 1), [1] * (amount - 1)
    while spare > 0:
        candidates = [i for i in range(amount - 1) if given[i] < reach]
        pool, remaining = sum([loads[i] for i in candidates]), spare
        for i in candidates:
            more = min(reach - given[i], max(1, remaining * loads[i] // pool), spare)
            given[i] = given[i] + more
            spare = spare - more
    return np.array([reach] + given)


def uneven_parts(rng, count, total, limit, slope):
    if count == 2:
        one = jax.random.randint(rng, (), max(1, total - limit), min(limit, total - 1) + 1)
        return jnp.stack([one, total - one])
    sizes = jnp.asarray(profile(count, total, limit, slope), jnp.int32)
    twos = (count - 1) // 2
    donor, sink = sizes[1:1 + 2 * twos:2], sizes[2:2 + 2 * twos:2]
    slack = jnp.minimum(donor - 1, limit - sink)
    shifted = jax.random.randint(jax.random.fold_in(rng, 1), (twos,), 0, 1 << 20) % (slack + 1)
    sizes = sizes.at[1:1 + 2 * twos:2].set(donor - shifted).at[2:2 + 2 * twos:2].set(sink + shifted)
    return sizes[jax.random.permutation(jax.random.fold_in(rng, 2), count)]


def scatter_about(key, shape, spread, most, pieces=(), kind=jnp.bfloat16):
    values = spread * jax.random.normal(key, shape, jnp.float32)
    if pieces:
        values = values * level_of(key, shape, pieces, -0.22, 0.18)
    return jnp.clip(values, -most, most).astype(kind)


def setup_inputs(seed: int = 0) -> dict:
    arg_keys = jax.random.split(jax.random.key(seed), 12)
    queries = draw_queries(jax.random.fold_in(arg_keys[11], 71), 0)
    d_out = scatter_about(arg_keys[1], (TOKENS, Q_HEADS * HEAD_DIM), 8.0, 48.0, ((0, 32), (1, 4)))
    conv_keys = scatter_about(arg_keys[2], (TOKENS, KV_HEADS * HEAD_DIM), 2.0, 12.0, ((0, 32), (1, 4)))
    conv_values = scatter_about(arg_keys[3], (TOKENS, KV_HEADS * HEAD_DIM), 1.0, 6.0, ((0, 32), (1, 4)))
    segment_ids = jax.vmap(lambda own: jnp.searchsorted(jnp.cumsum(uneven_parts(own, max(2, TOK_DEV // 64), TOK_DEV, 3 * TOK_DEV // 4, 2)), jnp.arange(TOK_DEV), side="right"))(jax.random.split(arg_keys[4], (N_DP * N_REPLICA))).reshape((N_DP * N_REPLICA, TOK_DEV)).astype(jnp.int32)
    master_keys = draw_master_keys(jax.random.fold_in(arg_keys[11], 71), 0)
    master_values = draw_master_values(jax.random.fold_in(arg_keys[11], 71), 0)
    moment_keys = scatter_about(arg_keys[7], (P_SIZE, KV_HEADS * HEAD_DIM), 0.5, 3.0, ((0, 8), (1, 4)), jnp.float32)
    moment_values = scatter_about(arg_keys[8], (P_SIZE, KV_HEADS * HEAD_DIM), 0.5, 3.0, ((0, 8), (1, 4)), jnp.float32)
    second_keys = jnp.clip(jnp.exp(math.log(1.0) - 4.6051702 * jax.random.uniform(arg_keys[9], (P_SIZE, KV_HEADS * HEAD_DIM), jnp.float32) ** level_of(arg_keys[9], (P_SIZE, KV_HEADS * HEAD_DIM), ((0, 8), (1, 4)), -0.2, 0.2)), 0.01, 1.0)
    second_values = jnp.clip(jnp.exp(math.log(1.0) - 4.6051702 * jax.random.uniform(arg_keys[10], (P_SIZE, KV_HEADS * HEAD_DIM), jnp.float32) ** level_of(arg_keys[10], (P_SIZE, KV_HEADS * HEAD_DIM), ((0, 8), (1, 4)), -0.2, 0.2)), 0.01, 1.0)
    return {"queries": queries, "d_out": d_out, "conv_keys": conv_keys, "conv_values": conv_values, "segment_ids": segment_ids, "master_keys": master_keys, "master_values": master_values, "moment_keys": moment_keys, "moment_values": moment_values, "second_keys": second_keys, "second_values": second_values}


BETA_ONE = 0.9
BETA_TWO = 0.95
LEARN_RATE = 0.05
WEIGHT_DECAY = 0.1
EPSILON = 1e-08

def attend_block(query_rows, grad_rows, own_keys, own_values, cart_keys, cart_values, visible):
    tokens_here, head_dim = own_keys.shape
    heads_here = query_rows.shape[1] // head_dim
    factor = head_dim ** (-0.5)
    flat_query = query_rows.reshape(tokens_here * heads_here, head_dim)
    flat_grad = grad_rows.reshape(tokens_here * heads_here, head_dim)
    cart_scores = jnp.dot(flat_query, cart_keys.T, preferred_element_type=jnp.float32) * factor
    own_scores = jnp.dot(flat_query, own_keys.T, preferred_element_type=jnp.float32) * factor
    own_scores = own_scores.reshape(tokens_here, heads_here, tokens_here)
    own_scores = jnp.where(visible[:, None, :], own_scores, -jnp.inf).reshape(tokens_here * heads_here, tokens_here)
    highest = jnp.maximum(lax.optimization_barrier(jnp.max(cart_scores, axis=1)), lax.optimization_barrier(jnp.max(own_scores, axis=1)))[:, None]
    cart_exp = jnp.exp(cart_scores - highest)
    own_exp = jnp.exp(own_scores - highest)
    denominator = lax.optimization_barrier(jnp.sum(cart_exp, axis=1, keepdims=True)) + lax.optimization_barrier(jnp.sum(own_exp, axis=1, keepdims=True))
    cart_probs = cart_exp / denominator
    own_probs = own_exp / denominator
    cart_dprob = jnp.dot(flat_grad, cart_values.T, preferred_element_type=jnp.float32)
    own_dprob = jnp.dot(flat_grad, own_values.T, preferred_element_type=jnp.float32)
    centre = lax.optimization_barrier(jnp.sum(cart_probs * cart_dprob, axis=1, keepdims=True)) + lax.optimization_barrier(jnp.sum(own_probs * own_dprob, axis=1, keepdims=True))
    cart_dscore = (cart_probs * (cart_dprob - centre)).astype(jnp.bfloat16)
    contract = (((0,), (0,)), ((), ()))
    grad_values = lax.dot_general(cart_probs.astype(jnp.bfloat16), flat_grad, contract, preferred_element_type=jnp.float32)
    grad_keys = lax.dot_general(cart_dscore, flat_query, contract, preferred_element_type=jnp.float32) * factor
    return (grad_keys, grad_values)

def device_grads(queries, d_out, conv_keys, conv_values, cart_keys, cart_values, segments):
    tokens_here = conv_keys.shape[0]
    head_dim = HEAD_DIM
    group_size = Q_HEADS // KV_HEADS
    half_size = group_size // 2
    kv_local = conv_keys.shape[1] // head_dim
    places = jnp.arange(tokens_here, dtype=jnp.int32)
    visible = (segments[:, None] == segments[None, :]) & (places[None, :] <= places[:, None])
    key_parts = []
    value_parts = []
    for kv_head in range(kv_local):
        col_lo = kv_head * head_dim
        col_hi = col_lo + head_dim
        key_sum = jnp.zeros((cart_keys.shape[0], head_dim), jnp.float32)
        value_sum = jnp.zeros((cart_keys.shape[0], head_dim), jnp.float32)
        for which_half in range(2):
            start_col = (kv_head * group_size + which_half * half_size) * head_dim
            end_col = start_col + half_size * head_dim
            grad_keys, grad_values = attend_block(queries[:, start_col:end_col], d_out[:, start_col:end_col], conv_keys[:, col_lo:col_hi], conv_values[:, col_lo:col_hi], cart_keys[:, col_lo:col_hi], cart_values[:, col_lo:col_hi], visible)
            key_sum = key_sum + grad_keys
            value_sum = value_sum + grad_values
        key_parts.append(key_sum)
        value_parts.append(value_sum)
    return (jnp.concatenate(key_parts, axis=1), jnp.concatenate(value_parts, axis=1))

def adamw_step(param, moment, second, grad):
    moment_new = BETA_ONE * moment + (1.0 - BETA_ONE) * grad
    second_new = BETA_TWO * second + (1.0 - BETA_TWO) * grad * grad
    moment_hat = moment_new / (1.0 - BETA_ONE ** STEP)
    second_hat = second_new / (1.0 - BETA_TWO ** STEP)
    param_new = param - LEARN_RATE * (moment_hat / (jnp.sqrt(second_hat) + EPSILON) + WEIGHT_DECAY * param)
    return (param_new, moment_new, second_new)

def reference(queries, d_out, conv_keys, conv_values, segment_ids, master_keys, master_values, moment_keys, moment_values, second_keys, second_values):
    cart_keys = master_keys.astype(jnp.bfloat16)
    cart_values = master_values.astype(jnp.bfloat16)
    blocks = segment_ids.shape[0]
    items = (queries.reshape(blocks, TOK_DEV, queries.shape[1]), d_out.reshape(blocks, TOK_DEV, d_out.shape[1]), conv_keys.reshape(blocks, TOK_DEV, conv_keys.shape[1]), conv_values.reshape(blocks, TOK_DEV, conv_values.shape[1]), segment_ids)

    def visit(carry, item):
        grad_keys, grad_values = device_grads(item[0], item[1], item[2], item[3], cart_keys, cart_values, item[4])
        return ((carry[0] + grad_keys, carry[1] + grad_values), None)
    zeros = jnp.zeros(master_keys.shape, jnp.float32)
    (grad_keys, grad_values), unused = lax.scan(visit, (zeros, zeros), items)
    new_master_keys, new_moment_keys, new_second_keys = adamw_step(master_keys, moment_keys, second_keys, grad_keys)
    new_master_values, new_moment_values, new_second_values = adamw_step(master_values, moment_values, second_values, grad_values)
    served_keys = new_master_keys.astype(jnp.bfloat16)
    served_values = new_master_values.astype(jnp.bfloat16)
    return (new_master_keys, new_master_values, new_moment_keys, new_moment_values, new_second_keys, new_second_values, served_keys, served_values, grad_keys, grad_values)
```

```python
import functools

import jax
import jax.numpy as jnp
from jax import lax
from jax.experimental import pallas as pl
from jax.experimental.pallas import tpu as pltpu
from jax.sharding import PartitionSpec as P

Q_HEADS = 64
KV_HEADS = 8
HEAD = 128
GROUP = Q_HEADS // KV_HEADS
TOK = 256
STEP = 20
BETA_ONE = 0.9
BETA_TWO = 0.95
LEARN_RATE = 0.05
WEIGHT_DECAY = 0.1
EPSILON = 1e-08
SCALE = HEAD**-0.5
LOG2E = 1.4426950408889634
NT = (((1,), (1,)), ((), ()))
F32 = jnp.float32
BF16 = jnp.bfloat16


OFFSETS = ((0, 0), (0, 1), (0, 3), (0, 2), (1, 0), (1, 1), (1, 3), (1, 2))


def attend_kernel(hp, ck, seg_ref, q_ref, do_ref, ko_ref, vo_ref, *refs):
    blocks, refs = refs[:8], refs[8:]
    outs, refs = refs[:8], refs[8:]
    k_ref, v_ref, s_ref, p_ref, dp_ref, dk_acc, dv_acc, sems = refs
    share = blocks[0].shape[0]
    keys = k_ref.shape[0]
    rows = hp * TOK
    steps = GROUP // hp
    chunks = keys // ck
    c = SCALE * LOG2E

    loads = [[], []]
    for b in range(8):
        for side, dst in enumerate((k_ref, v_ref)):
            load = pltpu.make_async_copy(
                blocks[b].at[:, pl.ds(side * HEAD, HEAD)],
                dst.at[pl.ds(b * share, share), :],
                sems.at[2 * b + side],
            )
            load.start()
            loads[side].append(load)

    def cols(ref, step):
        parts = [ref[:, (step * hp + j) * HEAD : (step * hp + j + 1) * HEAD] for j in range(hp)]
        return jnp.concatenate(parts, axis=0)

    def fold(x):
        return x.reshape(x.shape[0] // 8, 8, rows)

    seg_row = jnp.broadcast_to(seg_ref[...].astype(F32), (TOK, TOK))
    u = lax.broadcasted_iota(jnp.int32, (TOK, TOK), 0)
    t = lax.broadcasted_iota(jnp.int32, (TOK, TOK), 1)
    seen = (seg_row == seg_row.T) & (u <= t)

    def own_scores(step):
        s = lax.dot_general(ko_ref[...], cols(q_ref, step), NT, preferred_element_type=F32)
        parts = [jnp.where(seen, s[:, j * TOK : (j + 1) * TOK], -jnp.inf) for j in range(hp)]
        return jnp.concatenate(parts, axis=1)

    def spread(x, op):
        return jnp.broadcast_to(op(x, axis=0, keepdims=True), x.shape)

    state = {}
    for tick in range(steps + 2):
        one, two, three = tick, tick - 1, tick - 2
        run1, run2, run3 = one < steps, 0 <= two < steps, 0 <= three < steps
        init = []
        if run1:
            q1 = cols(q_ref, one)
            own = own_scores(one)
            init.append(jnp.max(fold(own), axis=0))
        if run2:
            mc = spread(state["m"], jnp.max) * c
            d2 = cols(do_ref, two)
            own_p = jnp.exp2(fold(state["own"]) * c - mc[None])
            own_dp = fold(lax.dot_general(vo_ref[...], d2, NT, preferred_element_type=F32))
            init.append(jnp.sum(own_p, axis=0))
            init.append(jnp.sum(own_p * own_dp, axis=0))
        if run3:
            inv = 1.0 / spread(state["l"], jnp.sum)
            centre = spread(state["c"], jnp.sum) * inv
            q3, d3 = cols(q_ref, three), cols(do_ref, three)
        if tick < 2:
            for load in loads[tick]:
                load.wait()

        def chunk(at, carry):
            out = []
            if run3:
                p = fold(p_ref[at, :]) * inv[None]
                ds = p * (fold(dp_ref[at, :]) - centre[None])
                p = p.reshape(ck, rows).astype(BF16)
                ds = ds.reshape(ck, rows).astype(BF16)
                gv = jnp.dot(p, d3, preferred_element_type=F32)
                gk = jnp.dot(ds, q3, preferred_element_type=F32)
                if three > 0:
                    gv = dv_acc[at, :] + gv
                    gk = dk_acc[at, :] + gk
                dv_acc[at, :] = gv
                dk_acc[at, :] = gk
            n = int(run1)
            if run2:
                p = jnp.exp2(fold(s_ref[at, :]) * c - mc[None])
                dp = lax.dot_general(v_ref[at, :], d2, NT, preferred_element_type=F32)
                total = carry[n] + jnp.sum(p, axis=0)
                centred = carry[n + 1] + jnp.sum(p * fold(dp), axis=0)
                p_ref[at, :] = p.reshape(ck, rows)
                dp_ref[at, :] = dp
            if run1:
                s = lax.dot_general(k_ref[at, :], q1, NT, preferred_element_type=F32)
                s_ref[at, :] = s
                out.append(jnp.maximum(carry[0], jnp.max(fold(s), axis=0)))
            if run2:
                out += [total, centred]
            return tuple(out)

        def body(i, carry):
            return chunk(pl.ds(pl.multiple_of(i * ck, ck), ck), carry)

        res = list(lax.fori_loop(0, chunks, body, tuple(init)))
        if run1:
            state["own"], state["m"] = own, res.pop(0)
        if run2:
            state["l"], state["c"] = res
    for b in range(8):
        at = pl.ds(b * share, share)
        outs[b][:, :HEAD] = (dk_acc[at, :] * SCALE).astype(BF16)
        outs[b][:, HEAD:] = dv_acc[at, :].astype(BF16)


def attend(group, seg, queries, d_out, conv_keys, conv_values, blocks, hp=2, ck=2048):
    share = blocks[0].shape[0]
    keys = 8 * share
    rows = hp * TOK
    vm = pl.BlockSpec(memory_space=pltpu.VMEM)
    wide = pl.BlockSpec((TOK, GROUP * HEAD), lambda i: (0, group))
    slim = pl.BlockSpec((TOK, HEAD), lambda i: (0, group))
    return pl.pallas_call(
        functools.partial(attend_kernel, hp, ck),
        grid=(1,),
        out_shape=[jax.ShapeDtypeStruct((share, 2 * HEAD), BF16)] * 8,
        in_specs=[pl.BlockSpec((1, TOK), lambda i: (0, 0)), wide, wide, slim, slim]
        + [pl.BlockSpec(memory_space=pl.ANY)] * 8,
        out_specs=[pl.BlockSpec((share, 2 * HEAD), lambda i: (0, 0))] * 8,
        scratch_shapes=[pltpu.VMEM((keys, HEAD), BF16)] * 2
        + [pltpu.VMEM((keys, rows), F32)] * 3
        + [pltpu.VMEM((keys, HEAD), F32)] * 2
        + [pltpu.SemaphoreType.DMA((16,))],
        cost_estimate=pl.CostEstimate(
            flops=8 * GROUP * TOK * keys * HEAD,
            bytes_accessed=8 << 20,
            transcendentals=GROUP * TOK * keys,
        ),
        compiler_params=pltpu.CompilerParams(vmem_limit_bytes=56 << 20),
        name="attend",
    )(seg, queries, d_out, conv_keys, conv_values, *blocks)


def fetch(value, offset):
    z, y = offset
    pairs = [(s, ((s // 4 + z) % 2) * 4 + (s % 4 - y) % 4) for s in range(8)]
    return lax.ppermute(value, "dp", pairs)


def deliver(value, offset):
    z, y = offset
    pairs = [(s, ((s // 4 + z) % 2) * 4 + (s % 4 + y) % 4) for s in range(8)]
    return lax.ppermute(value, "dp", pairs)


def turn(value, by):
    return lax.ppermute(value, "replica", [(s, (s + by) % 4) for s in range(4)])


def gather(own):
    return [own] + [fetch(own, o) for o in OFFSETS[1:]]


def scatter_sum(parts):
    got = [parts[0]] + [deliver(p, o) for p, o in zip(parts[1:], OFFSETS[1:])]
    got = [g.astype(F32) for g in got]
    return ((got[0] + got[1]) + (got[2] + got[3])) + ((got[4] + got[5]) + (got[6] + got[7]))


def replica_sum(value):
    own = value.astype(BF16)
    a, b, c = turn(own, 1), turn(own, 2), turn(own, 3)
    own, a, b, c = (x.astype(F32) for x in (own, a, b, c))
    return (own + b) + (a + c)


def adamw_step(param, moment, second, grad):
    moment_new = BETA_ONE * moment + (1.0 - BETA_ONE) * grad
    second_new = BETA_TWO * second + (1.0 - BETA_TWO) * grad * grad
    moment_hat = moment_new / (1.0 - BETA_ONE**STEP)
    second_hat = second_new / (1.0 - BETA_TWO**STEP)
    param_new = param - LEARN_RATE * (
        moment_hat / (jnp.sqrt(second_hat) + EPSILON) + WEIGHT_DECAY * param
    )
    return (param_new, moment_new, second_new)


def place_kernel(rows_ref, *refs):
    blocks, keys_ref, values_ref = refs[:8], refs[8], refs[9]
    hold, sems_in, sems_out = refs[10:]
    share = blocks[0].shape[0]
    half = keys_ref.shape[1]
    loads = [pltpu.make_async_copy(blocks[b], hold.at[b], sems_in.at[b]) for b in range(8)]
    for load in loads:
        load.start()
    stores = []
    for b in range(8):
        loads[b].wait()
        at = pl.ds(pl.multiple_of(rows_ref[b], share), share)
        for side, out in enumerate((keys_ref, values_ref)):
            store = pltpu.make_async_copy(
                hold.at[b, :, pl.ds(side * half, half)], out.at[at, :], sems_out.at[2 * b + side]
            )
            store.start()
            stores.append(store)
    for store in stores:
        store.wait()


def place(rows, blocks):
    share, wide = blocks[0].shape
    out = jax.ShapeDtypeStruct((8 * share, wide // 2), BF16)
    anywhere = pl.BlockSpec(memory_space=pl.ANY)
    return pl.pallas_call(
        place_kernel,
        out_shape=[out, out],
        in_specs=[pl.BlockSpec(memory_space=pltpu.SMEM)] + [anywhere] * 8,
        out_specs=[anywhere] * 2,
        scratch_shapes=[
            pltpu.VMEM((8, share, wide), BF16),
            pltpu.SemaphoreType.DMA((8,)),
            pltpu.SemaphoreType.DMA((16,)),
        ],
        name="place",
    )(rows, *blocks)


def per_device(
    queries,
    d_out,
    conv_keys,
    conv_values,
    segment_ids,
    master_keys,
    master_values,
    moment_keys,
    moment_values,
    second_keys,
    second_values,
):
    share = master_keys.shape[0]

    def own_block(head):
        at = slice(head * HEAD, (head + 1) * HEAD)
        return jnp.concatenate([master_keys[:, at], master_values[:, at]], axis=1).astype(BF16)

    def attention(group, blocks):
        return attend(group, segment_ids, queries, d_out, conv_keys, conv_values, blocks)

    first = gather(own_block(0))
    *first, later = lax.optimization_barrier((*first, own_block(1)))
    parts_first = attention(0, first)
    second = gather(later)
    parts_second = attention(1, second)
    sum_first = replica_sum(scatter_sum(parts_first))
    sum_second = replica_sum(scatter_sum(parts_second))
    grad_keys = jnp.concatenate([sum_first[:, :HEAD], sum_second[:, :HEAD]], axis=1)
    grad_values = jnp.concatenate([sum_first[:, HEAD:], sum_second[:, HEAD:]], axis=1)
    new_master_keys, new_moment_keys, new_second_keys = adamw_step(
        master_keys, moment_keys, second_keys, grad_keys
    )
    new_master_values, new_moment_values, new_second_values = adamw_step(
        master_values, moment_values, second_values, grad_values
    )
    served = jnp.concatenate([new_master_keys, new_master_values], axis=1).astype(BF16)
    me = lax.axis_index("dp")
    rows = jnp.stack([((me // 4 + z) % 2) * 4 + (me % 4 + y) % 4 for z, y in OFFSETS]) * share
    served_keys, served_values = place(rows.astype(jnp.int32), gather(served))
    return (
        new_master_keys,
        new_master_values,
        new_moment_keys,
        new_moment_values,
        new_second_keys,
        new_second_values,
        served_keys,
        served_values,
        grad_keys,
        grad_values,
    )


def solution(mesh):
    tokens = P(("dp", "replica"), "tensor")
    shard = P("dp", "tensor")
    served = P(None, "tensor")
    return jax.shard_map(
        per_device,
        mesh=mesh,
        in_specs=(tokens,) * 4 + (P(("dp", "replica"), None),) + (shard,) * 6,
        out_specs=(shard,) * 6 + (served,) * 2 + (shard,) * 2,
        check_vma=False,
    )
```

```python
import functools

import jax
import jax.numpy as jnp
from jax import lax
from jax.experimental import pallas as pl
from jax.experimental.pallas import tpu as pltpu
from jax.sharding import PartitionSpec as P


Q_HEADS = 64
KV_HEADS = 8
HEAD = 128
GROUP = Q_HEADS // KV_HEADS
TOK = 256
STEP = 20
BETA_ONE = 0.9
BETA_TWO = 0.95
LEARN_RATE = 0.05
WEIGHT_DECAY = 0.1
EPSILON = 1e-08
SCALE = HEAD**-0.5
LOG2E = 1.4426950408889634
NT = (((1,), (1,)), ((), ()))
F32 = jnp.float32
BF16 = jnp.bfloat16


OFFSETS = ((0, 0), (0, 1), (0, 3), (0, 2), (1, 0), (1, 1), (1, 3), (1, 2))


def block_rows(share, absolute):
    if absolute:
        return [b * share for b in range(8)]
    me = lax.axis_index("dp")
    far, mine = lax.div(me, 4), lax.rem(me, 4)
    return [(lax.rem(far + z, 2) * 4 + lax.rem(mine + y, 4)) * share for z, y in OFFSETS]


def quarter_rows(size):
    here = lax.axis_index("replica")
    return [lax.rem(here + j, 4) * size for j in range(4)]


def attend_kernel(hp, ck, pieces, absolute, seg_ref, q_ref, do_ref, ko_ref, vo_ref, *refs):
    count = 1 + max(p[0] for p in pieces)
    arrays, refs = refs[:count], refs[count:]
    sends, refs = refs[:5], refs[5:]
    k_ref, v_ref, s_ref, p_ref, dp_ref, dk_acc, dv_acc, sems = refs
    keys = k_ref.shape[0]
    rows = hp * TOK
    steps = GROUP // hp
    chunks = keys // ck
    c = SCALE * LOG2E

    starts = block_rows(keys // 8, absolute)
    loads = [[], []]
    for side, dst in enumerate((k_ref, v_ref)):
        for n, (array, src, size, block, low) in enumerate(pieces):
            at = pl.multiple_of(starts[block] + low, size)
            load = pltpu.make_async_copy(
                arrays[array].at[pl.ds(src, size), pl.ds(side * HEAD, HEAD)],
                dst.at[pl.ds(at, size), :],
                sems.at[side * len(pieces) + n],
            )
            load.start()
            loads[side].append(load)

    def cols(ref, step):
        parts = []
        for j in range(hp):
            at = (step * hp + j) * HEAD
            parts.append(ref[:, pl.ds(pl.multiple_of(at, HEAD), HEAD)])
        return jnp.concatenate(parts, axis=0)

    def fold(x):
        return x.reshape(x.shape[0] // 8, 8, rows)

    seg_row = jnp.broadcast_to(seg_ref[...].astype(F32), (TOK, TOK))
    u = lax.broadcasted_iota(jnp.int32, (TOK, TOK), 0)
    t = lax.broadcasted_iota(jnp.int32, (TOK, TOK), 1)
    seen = (seg_row == seg_row.T) & (u <= t)

    def spread(x, op):
        return jnp.broadcast_to(op(x, axis=0, keepdims=True), x.shape)

    def tick(at, one, two, three, state):
        highest, total, centred = state
        init = []
        if one:
            q1 = cols(q_ref, at)
            own = lax.dot_general(ko_ref[...], q1, NT, preferred_element_type=F32)
            parts = [jnp.where(seen, own[:, j * TOK : (j + 1) * TOK], -jnp.inf) for j in range(hp)]
            own = jnp.concatenate(parts, axis=1)
            init.append(jnp.max(fold(own), axis=0))
        if two:
            mc = spread(highest, jnp.max) * c
            q2, d2 = cols(q_ref, at - 1), cols(do_ref, at - 1)
            own2 = lax.dot_general(ko_ref[...], q2, NT, preferred_element_type=F32)
            parts = [jnp.where(seen, own2[:, j * TOK : (j + 1) * TOK], -jnp.inf) for j in range(hp)]
            own2 = jnp.concatenate(parts, axis=1)
            own_p = jnp.exp2(fold(own2) * c - mc[None])
            own_dp = fold(lax.dot_general(vo_ref[...], d2, NT, preferred_element_type=F32))
            init.append(jnp.sum(own_p, axis=0))
            init.append(jnp.sum(own_p * own_dp, axis=0))
        if three:
            inv = 1.0 / spread(total, jnp.sum)
            centre = spread(centred, jnp.sum) * inv
            q3, d3 = cols(q_ref, at - 2), cols(do_ref, at - 2)

        def body(i, carry):
            out = []
            here = pl.ds(pl.multiple_of(i * ck, ck), ck)
            if three:
                p = fold(p_ref[here, :]) * inv[None]
                ds = p * (fold(dp_ref[here, :]) - centre[None])
                p = p.reshape(ck, rows).astype(BF16)
                ds = ds.reshape(ck, rows).astype(BF16)
                dv_acc[here, :] += jnp.dot(p, d3, preferred_element_type=F32)
                dk_acc[here, :] += jnp.dot(ds, q3, preferred_element_type=F32)
            n = int(one)
            if two:
                p = jnp.exp2(fold(s_ref[here, :]) * c - mc[None])
                dp = lax.dot_general(v_ref[here, :], d2, NT, preferred_element_type=F32)
                total_now = carry[n] + jnp.sum(p, axis=0)
                centred_now = carry[n + 1] + jnp.sum(p * fold(dp), axis=0)
                p_ref[here, :] = p.reshape(ck, rows)
                dp_ref[here, :] = dp
            if one:
                s = lax.dot_general(k_ref[here, :], q1, NT, preferred_element_type=F32)
                s_ref[here, :] = s
                out.append(jnp.maximum(carry[0], jnp.max(fold(s), axis=0)))
            else:
                out.append(highest)
            if two:
                out += [total_now, centred_now]
            else:
                out += [total, centred]
            return tuple(out)

        full = (init[0] if one else highest,) + (tuple(init[int(one) :]) if two else (total, centred))

        def step(i, carry):
            picked = ([carry[0]] if one else []) + (list(carry[1:]) if two else [])
            return body(i, picked)

        return lax.fori_loop(0, chunks, step, full)

    none = jnp.zeros((8, rows), F32)
    state = (none, none, none)
    for load in loads[0]:
        load.wait()
    state = tick(0, True, False, False, state)
    dk_acc[...] = jnp.zeros_like(dk_acc)
    dv_acc[...] = jnp.zeros_like(dv_acc)
    for load in loads[1]:
        load.wait()
    state = tick(1, True, True, False, state)
    state = lax.fori_loop(2, steps, lambda at, st: tick(at, True, True, True, st), state)
    state = tick(steps, False, True, True, state)
    tick(steps + 1, False, False, True, state)
    send_keys, send_values = sends[0], sends[1:]
    blocks, _, size, _ = send_keys.shape
    turns = quarter_rows(size)
    for j in range(4):
        for block in range(blocks):
            here = pl.ds(pl.multiple_of(block * 4 * size + turns[j], size), size)
            send_keys[block, j] = (dk_acc[here, :] * SCALE).astype(BF16)
            send_values[j][block] = dv_acc[here, :].astype(BF16)


def attend(group, absolute, seg, queries, d_out, conv_keys, conv_values, arrays, pieces, hp=2, ck=2048):
    keys = sum(p[2] for p in pieces)
    rows = hp * TOK
    anywhere = pl.BlockSpec(memory_space=pltpu.HBM)
    wide = pl.BlockSpec((TOK, GROUP * HEAD), lambda i: (0, group))
    slim = pl.BlockSpec((TOK, HEAD), lambda i: (0, group))
    return pl.pallas_call(
        functools.partial(attend_kernel, hp, ck, pieces, absolute),
        grid=(1,),
        out_shape=[
            jax.ShapeDtypeStruct((8, 4, keys // 32, HEAD), BF16),
            *[jax.ShapeDtypeStruct((8, keys // 32, HEAD), BF16)] * 4,
        ],
        in_specs=[pl.BlockSpec((1, TOK), lambda i: (0, 0)), wide, wide, slim, slim]
        + [anywhere] * len(arrays),
        out_specs=[
            pl.BlockSpec((8, 4, keys // 32, HEAD), lambda i: (0, 0, 0, 0)),
            *[pl.BlockSpec((8, keys // 32, HEAD), lambda i: (0, 0, 0))] * 4,
        ],
        scratch_shapes=[pltpu.VMEM((keys, HEAD), BF16)] * 2
        + [pltpu.VMEM((keys, rows), F32)] * 3
        + [pltpu.VMEM((keys, HEAD), F32)] * 2
        + [pltpu.SemaphoreType.DMA((2 * len(pieces),))],
        cost_estimate=pl.CostEstimate(
            flops=8 * GROUP * TOK * keys * HEAD,
            bytes_accessed=8 << 20,
            transcendentals=GROUP * TOK * keys,
        ),
        compiler_params=pltpu.CompilerParams(vmem_limit_bytes=56 << 20),
        name="attend",
    )(seg, queries, d_out, conv_keys, conv_values, *arrays)


def fetch(value, offset):
    z, y = offset
    pairs = [(s, ((s // 4 + z) % 2) * 4 + (s % 4 - y) % 4) for s in range(8)]
    return lax.ppermute(value, "dp", pairs)


def relay_gather(own):
    half = own.shape[0] // 2
    far = fetch(own, (1, 0))
    up, down = fetch(own, (0, 1)), fetch(own, (0, 3))
    up, down, far = lax.optimization_barrier((up, down, far))
    from_far = fetch(jnp.concatenate([up[half:], down[half:]]), (1, 0))
    from_up = fetch(jnp.concatenate([up[:half], far[:half]]), (0, 1))
    from_down = fetch(jnp.concatenate([down[half:], far[:half]]), (0, 3))
    from_up, from_down, from_far = lax.optimization_barrier((from_up, from_down, from_far))
    last_far = fetch(from_down[:half], (1, 0))
    last_up = fetch(from_up[half:], (0, 1))
    return own, up, down, far, from_up, from_down, from_far, last_up, last_far


def relay_pieces(share):
    half = share // 2
    whole = [(0, 0, share, 0, 0), (1, 0, share, 1, 0), (2, 0, share, 2, 0), (3, 0, share, 4, 0)]
    halves = [
        (4, 0, half, 3, 0),
        (4, half, half, 5, 0),
        (5, 0, half, 3, half),
        (5, half, half, 6, 0),
        (6, 0, half, 5, half),
        (6, half, half, 6, half),
        (7, 0, half, 7, 0),
        (8, 0, half, 7, half),
    ]
    return whole + halves


def turn(value, by):
    return lax.ppermute(value, "replica", [(s, (s + by) % 4) for s in range(4)])


def total(parts):
    parts = [p.astype(F32) for p in parts]
    while len(parts) > 1:
        parts = [a + b for a, b in zip(parts[::2], parts[1::2])]
    return parts[0]


def dp_sum(parts):
    got = lax.all_to_all(parts, "dp", 0, 0, tiled=True)
    return total([got[i] for i in range(8)])


def replica_sum(parts):
    return total([parts[0]] + [turn(parts[j], j) for j in (1, 3, 2)])


def adamw_step(param, moment, second, grad):
    moment_new = BETA_ONE * moment + (1.0 - BETA_ONE) * grad
    second_new = BETA_TWO * second + (1.0 - BETA_TWO) * grad * grad
    moment_hat = moment_new / (1.0 - BETA_ONE**STEP)
    second_hat = second_new / (1.0 - BETA_TWO**STEP)
    param_new = param - LEARN_RATE * (
        moment_hat / (jnp.sqrt(second_hat) + EPSILON) + WEIGHT_DECAY * param
    )
    return (param_new, moment_new, second_new)


def place_kernel(pieces, skip, *refs):
    count = 1 + max(p[0] for p in pieces)
    arrays, refs = refs[:count], refs[count + skip :]
    keys_ref, values_ref, hold, sems_in, sems_out = refs
    half = keys_ref.shape[1]
    starts = block_rows(keys_ref.shape[0] // 8, False)
    loads, at = [], 0
    for n, (array, src, size, _, _) in enumerate(pieces):
        load = pltpu.make_async_copy(
            arrays[array].at[pl.ds(src, size), :], hold.at[pl.ds(at, size), :], sems_in.at[n]
        )
        load.start()
        loads.append((load, at))
        at += size
    stores = []
    for n, (_, _, size, block, low) in enumerate(pieces):
        load, at = loads[n]
        load.wait()
        to = pl.multiple_of(starts[block] + low, size)
        for side, out in enumerate((keys_ref, values_ref)):
            store = pltpu.make_async_copy(
                hold.at[pl.ds(at, size), pl.ds(side * half, half)],
                out.at[pl.ds(to, size), :],
                sems_out.at[2 * n + side],
            )
            store.start()
            stores.append(store)
    for store in stores:
        store.wait()


def place(arrays, pieces, keys, started=()):
    rows, wide = sum(p[2] for p in pieces), arrays[0].shape[1]
    out = jax.ShapeDtypeStruct((keys, wide // 2), BF16)
    anywhere = pl.BlockSpec(memory_space=pltpu.HBM)
    first = len(arrays)
    return pl.pallas_call(
        functools.partial(place_kernel, pieces, len(started)),
        out_shape=[out, out],
        in_specs=[anywhere] * (len(arrays) + len(started)),
        out_specs=[anywhere] * 2,
        input_output_aliases={first + i: i for i in range(len(started))},
        scratch_shapes=[
            pltpu.VMEM((rows, wide), BF16),
            pltpu.SemaphoreType.DMA((len(pieces),)),
            pltpu.SemaphoreType.DMA((2 * len(pieces),)),
        ],
        name="place",
    )(*arrays, *started)


def update_kernel(serve, *refs):
    grads, olds, outs = refs[:4], refs[4:10], refs[10:]
    size = grads[0].shape[0]
    half = grads[0].shape[1] // 2
    turns = quarter_rows(size)
    for j in range(4):
        at = pl.ds(pl.multiple_of(turns[j], size), size)
        for side in range(2):
            cols = slice(side * half, (side + 1) * half)
            grad = grads[j][:, cols].astype(F32)
            new = adamw_step(*[olds[2 * n + side][at, :] for n in range(3)], grad)
            if serve:
                outs[0][at, cols] = new[0].astype(BF16)
            else:
                for n in range(3):
                    outs[2 * n + side][at, :] = new[n]
                outs[6 + side][at, :] = grad


def update(serve, grads, olds):
    share, half = olds[0].shape
    vm = pl.BlockSpec(memory_space=pltpu.VMEM)
    shard = jax.ShapeDtypeStruct((share, half), F32)
    served = jax.ShapeDtypeStruct((share, 2 * half), BF16)
    outs = [served] if serve else [shard] * 8
    return pl.pallas_call(
        functools.partial(update_kernel, serve),
        out_shape=outs,
        in_specs=[vm] * 10,
        out_specs=[vm] * len(outs),
        cost_estimate=pl.CostEstimate(flops=0, bytes_accessed=8 << 20, transcendentals=0),
        name="serve" if serve else "update",
    )(*grads, *olds)


def per_device(
    queries,
    d_out,
    conv_keys,
    conv_values,
    segment_ids,
    master_keys,
    master_values,
    moment_keys,
    moment_values,
    second_keys,
    second_values,
):
    share = master_keys.shape[0]
    relayed = relay_pieces(share)

    def own_block(head):
        at = slice(head * HEAD, (head + 1) * HEAD)
        return jnp.concatenate([master_keys[:, at], master_values[:, at]], axis=1).astype(BF16)

    def attention(group, absolute, arrays, pieces):
        tokens = (segment_ids, queries, d_out, conv_keys, conv_values)
        return attend(group, absolute, *tokens, arrays, pieces)

    later = jnp.broadcast_to(own_block(1), (8, share, 2 * HEAD))
    first = relay_gather(own_block(0))
    *first, later = lax.optimization_barrier((*first, later))
    parts_first = attention(0, False, first, relayed)
    second = lax.all_to_all(later, "dp", 0, 0, tiled=True).reshape(8 * share, 2 * HEAD)
    parts_second = attention(
        1, True, [second], [(0, b * share, share, b, 0) for b in range(8)]
    )
    keys_sum = [dp_sum(parts[0]) for parts in (parts_first, parts_second)]
    values_sum = [replica_sum(parts_first[1:])]
    values_sum.append(replica_sum(parts_second[1:]))
    keys_low = jnp.concatenate(keys_sum, axis=2).astype(BF16)
    values_low = jnp.concatenate(values_sum, axis=2).astype(BF16)
    keys_quarter = replica_sum([keys_low[j] for j in range(4)])
    values_quarter = dp_sum(values_low)
    both = jnp.concatenate([keys_quarter, values_quarter], axis=1).astype(BF16)
    grads = [both] + [turn(both, -j) for j in (1, 2, 3)]
    olds = (master_keys, master_values, moment_keys, moment_values, second_keys, second_values)
    (served,) = update(True, grads, olds)
    *news, grad_keys, grad_values = update(False, grads, olds)
    arrays = relay_gather(served)
    started = ()
    for low, high in ((0, 4), (4, 7), (7, 9)):
        part = [(p[0] - low, *p[1:]) for p in relayed if low <= p[0] < high]
        started = place(arrays[low:high], part, 8 * share, started)
    return (*news, *started, grad_keys, grad_values)


def solution(mesh):
    tokens = P(("dp", "replica"), "tensor")
    shard = P("dp", "tensor")
    served = P(None, "tensor")
    return jax.shard_map(
        per_device,
        mesh=mesh,
        in_specs=(tokens,) * 4 + (P(("dp", "replica"), None),) + (shard,) * 6,
        out_specs=(shard,) * 6 + (served,) * 2 + (shard,) * 2,
        check_vma=False,
    )
```

```python
import functools

import jax
import jax.numpy as jnp
from jax import lax
from jax.experimental import pallas as pl
from jax.experimental.pallas import tpu as pltpu
from jax.sharding import PartitionSpec as P


Q_HEADS = 64
KV_HEADS = 8
HEAD = 128
GROUP = Q_HEADS // KV_HEADS
TOK = 256
STEP = 20
BETA_ONE = 0.9
BETA_TWO = 0.95
LEARN_RATE = 0.05
WEIGHT_DECAY = 0.1
EPSILON = 1e-08
SCALE = HEAD**-0.5
LOG2E = 1.4426950408889634
NT = (((1,), (1,)), ((), ()))
F32 = jnp.float32
BF16 = jnp.bfloat16


OFFSETS = ((0, 0), (0, 1), (0, 3), (0, 2), (1, 0), (1, 1), (1, 3), (1, 2))


def block_rows(share, absolute):
    if absolute:
        return [b * share for b in range(8)]
    me = lax.axis_index("dp")
    far, mine = lax.div(me, 4), lax.rem(me, 4)
    return [(lax.rem(far + z, 2) * 4 + lax.rem(mine + y, 4)) * share for z, y in OFFSETS]


def quarter_rows(size):
    here = lax.axis_index("replica")
    return [lax.rem(here + j, 4) * size for j in range(4)]


def attend_kernel(hp, ck, pieces, first, seg_ref, q_ref, do_ref, ko_ref, vo_ref, *refs):
    count = 1 + max(p[0] for p in pieces)
    arrays, refs = refs[:count], refs[count:]
    sends, refs = (refs[:1], refs[1:]) if first else (refs[:5], refs[5:])
    k_ref, v_ref, s_ref, p_ref, dp_ref, dk_acc, dv_acc, sems = refs
    keys = k_ref.shape[0]
    rows = hp * TOK
    steps = GROUP // hp
    chunks = keys // ck
    c = SCALE * LOG2E

    starts = block_rows(keys // 8, not first)
    loads = [[], []]
    for side, dst in enumerate((k_ref, v_ref)):
        for n, (array, src, size, block, low) in enumerate(pieces):
            at = pl.multiple_of(starts[block] + low, size)
            load = pltpu.make_async_copy(
                arrays[array].at[pl.ds(src, size), pl.ds(side * HEAD, HEAD)],
                dst.at[pl.ds(at, size), :],
                sems.at[side * len(pieces) + n],
            )
            load.start()
            loads[side].append(load)

    def cols(ref, step):
        parts = []
        for j in range(hp):
            at = (step * hp + j) * HEAD
            parts.append(ref[:, pl.ds(pl.multiple_of(at, HEAD), HEAD)])
        return jnp.concatenate(parts, axis=0)

    def fold(x):
        return x.reshape(x.shape[0] // 8, 8, rows)

    seg_row = jnp.broadcast_to(seg_ref[...].astype(F32), (TOK, TOK))
    u = lax.broadcasted_iota(jnp.int32, (TOK, TOK), 0)
    t = lax.broadcasted_iota(jnp.int32, (TOK, TOK), 1)
    seen = (seg_row == seg_row.T) & (u <= t)

    def spread(x, op):
        return jnp.broadcast_to(op(x, axis=0, keepdims=True), x.shape)

    def tick(at, one, two, three, state):
        highest, total, centred = state
        init = []
        if one:
            q1 = cols(q_ref, at)
            own = lax.dot_general(ko_ref[...], q1, NT, preferred_element_type=F32)
            parts = [jnp.where(seen, own[:, j * TOK : (j + 1) * TOK], -jnp.inf) for j in range(hp)]
            own = jnp.concatenate(parts, axis=1)
            init.append(jnp.max(fold(own), axis=0))
        if two:
            mc = spread(highest, jnp.max) * c
            q2, d2 = cols(q_ref, at - 1), cols(do_ref, at - 1)
            own2 = lax.dot_general(ko_ref[...], q2, NT, preferred_element_type=F32)
            parts = [jnp.where(seen, own2[:, j * TOK : (j + 1) * TOK], -jnp.inf) for j in range(hp)]
            own2 = jnp.concatenate(parts, axis=1)
            own_p = jnp.exp2(fold(own2) * c - mc[None])
            own_dp = fold(lax.dot_general(vo_ref[...], d2, NT, preferred_element_type=F32))
            init.append(jnp.sum(own_p, axis=0))
            init.append(jnp.sum(own_p * own_dp, axis=0))
        if three:
            inv = 1.0 / spread(total, jnp.sum)
            centre = spread(centred, jnp.sum) * inv
            q3, d3 = cols(q_ref, at - 2), cols(do_ref, at - 2)

        def body(i, carry):
            out = []
            here = pl.ds(pl.multiple_of(i * ck, ck), ck)
            if three:
                p = fold(p_ref[here, :]) * inv[None]
                ds = p * (fold(dp_ref[here, :]) - centre[None])
                p = p.reshape(ck, rows).astype(BF16)
                ds = ds.reshape(ck, rows).astype(BF16)
                dv_acc[here, :] += jnp.dot(p, d3, preferred_element_type=F32)
                dk_acc[here, :] += jnp.dot(ds, q3, preferred_element_type=F32)
            n = int(one)
            if two:
                p = jnp.exp2(fold(s_ref[here, :]) * c - mc[None])
                dp = lax.dot_general(v_ref[here, :], d2, NT, preferred_element_type=F32)
                total_now = carry[n] + jnp.sum(p, axis=0)
                centred_now = carry[n + 1] + jnp.sum(p * fold(dp), axis=0)
                p_ref[here, :] = p.reshape(ck, rows)
                dp_ref[here, :] = dp
            if one:
                s = lax.dot_general(k_ref[here, :], q1, NT, preferred_element_type=F32)
                s_ref[here, :] = s
                out.append(jnp.maximum(carry[0], jnp.max(fold(s), axis=0)))
            else:
                out.append(highest)
            if two:
                out += [total_now, centred_now]
            else:
                out += [total, centred]
            return tuple(out)

        full = (init[0] if one else highest,) + (tuple(init[int(one) :]) if two else (total, centred))

        def step(i, carry):
            picked = ([carry[0]] if one else []) + (list(carry[1:]) if two else [])
            return body(i, picked)

        return lax.fori_loop(0, chunks, step, full)

    none = jnp.zeros((8, rows), F32)
    state = (none, none, none)
    for load in loads[0]:
        load.wait()
    state = tick(0, True, False, False, state)
    dk_acc[...] = jnp.zeros_like(dk_acc)
    dv_acc[...] = jnp.zeros_like(dv_acc)
    for load in loads[1]:
        load.wait()
    state = tick(1, True, True, False, state)
    state = lax.fori_loop(2, steps, lambda at, st: tick(at, True, True, True, st), state)
    state = tick(steps, False, True, True, state)
    tick(steps + 1, False, False, True, state)
    blocks, _, size, _ = sends[0].shape
    turns = quarter_rows(size)
    offsets = block_rows(4 * size, False)
    for j in range(4):
        for block in range(blocks):
            here = pl.ds(pl.multiple_of(block * 4 * size + turns[j], size), size)
            sends[0][block, j, :, :HEAD] = (dk_acc[here, :] * SCALE).astype(BF16)
            if first:
                sends[0][block, j, :, HEAD:] = dv_acc[here, :].astype(BF16)
            else:
                there = pl.ds(pl.multiple_of(offsets[block] + turns[j], size), size)
                sends[1 + j][2 * (block % 4) + block // 4] = dv_acc[there, :].astype(BF16)


def attend(group, first, seg, queries, d_out, conv_keys, conv_values, arrays, pieces, hp=2, ck=2048):
    keys = sum(p[2] for p in pieces)
    rows = hp * TOK
    anywhere = pl.BlockSpec(memory_space=pltpu.VMEM)
    wide = pl.BlockSpec((TOK, GROUP * HEAD), lambda i: (0, group))
    slim = pl.BlockSpec((TOK, HEAD), lambda i: (0, group))
    size = keys // 32
    sends = [(8, 4, size, 2 * HEAD)] if first else [(8, 4, size, HEAD)] + [(8, size, HEAD)] * 4
    return pl.pallas_call(
        functools.partial(attend_kernel, hp, ck, pieces, first),
        grid=(1,),
        out_shape=[jax.ShapeDtypeStruct(shape, BF16) for shape in sends],
        in_specs=[pl.BlockSpec((1, TOK), lambda i: (0, 0)), wide, wide, slim, slim]
        + [anywhere] * len(arrays),
        out_specs=[pl.BlockSpec(shape, lambda i, n=len(shape): (0,) * n) for shape in sends],
        scratch_shapes=[pltpu.VMEM((keys, HEAD), BF16)] * 2
        + [pltpu.VMEM((keys, rows), F32)] * 3
        + [pltpu.VMEM((keys, HEAD), F32)] * 2
        + [pltpu.SemaphoreType.DMA((2 * len(pieces),))],
        cost_estimate=pl.CostEstimate(
            flops=8 * GROUP * TOK * keys * HEAD,
            bytes_accessed=8 << 20,
            transcendentals=GROUP * TOK * keys,
        ),
        compiler_params=pltpu.CompilerParams(vmem_limit_bytes=50 << 20),
        name="attend",
    )(seg, queries, d_out, conv_keys, conv_values, *arrays)


def fetch(value, offset):
    z, y = offset
    pairs = [(s, ((s // 4 + z) % 2) * 4 + (s % 4 - y) % 4) for s in range(8)]
    return lax.ppermute(value, "dp", pairs)


def relay_gather(own):
    half = own.shape[0] // 2
    far = fetch(own, (1, 0))
    up, down = fetch(own, (0, 1)), fetch(own, (0, 3))
    up, down, far = lax.optimization_barrier((up, down, far))
    from_far = fetch(jnp.concatenate([up[half:], down[half:]]), (1, 0))
    from_up = fetch(jnp.concatenate([up[:half], far[:half]]), (0, 1))
    from_down = fetch(jnp.concatenate([down[half:], far[:half]]), (0, 3))
    from_up, from_down, from_far = lax.optimization_barrier((from_up, from_down, from_far))
    last_far = fetch(from_down[:half], (1, 0))
    last_up = fetch(from_up[half:], (0, 1))
    return own, up, down, far, from_up, from_down, from_far, last_up, last_far


def relay_pieces(share):
    half = share // 2
    whole = [(0, 0, share, 0, 0), (1, 0, share, 1, 0), (2, 0, share, 2, 0), (3, 0, share, 4, 0)]
    halves = [
        (4, 0, half, 3, 0),
        (4, half, half, 5, 0),
        (5, 0, half, 3, half),
        (5, half, half, 6, 0),
        (6, 0, half, 5, half),
        (6, half, half, 6, half),
        (7, 0, half, 7, 0),
        (8, 0, half, 7, half),
    ]
    return whole + halves


def deliver(value, offset):
    z, y = offset
    pairs = [(s, ((s // 4 + z) % 2) * 4 + (s % 4 + y) % 4) for s in range(8)]
    return lax.ppermute(value, "dp", pairs)


def lines_sum(parts):
    sent = [deliver(parts[2 * i : 2 * i + 2], OFFSETS[i]) for i in (1, 2, 3)]
    here, far = total([parts[:2], *sent])
    far = deliver(far.astype(BF16), (1, 0))
    return here + far.astype(F32)


def turn(value, by):
    return lax.ppermute(value, "replica", [(s, (s + by) % 4) for s in range(4)])


def total(parts):
    parts = [p.astype(F32) for p in parts]
    while len(parts) > 1:
        parts = [a + b for a, b in zip(parts[::2], parts[1::2])]
    return parts[0]


def dp_sum(parts):
    got = lax.all_to_all(parts, "dp", 0, 0, tiled=True)
    return total([got[i] for i in range(8)])


def replica_sum(parts):
    return total([parts[0]] + [turn(parts[j], j) for j in (1, 3, 2)])


def adamw_step(param, moment, second, grad):
    moment_new = BETA_ONE * moment + (1.0 - BETA_ONE) * grad
    second_new = BETA_TWO * second + (1.0 - BETA_TWO) * grad * grad
    moment_hat = moment_new / (1.0 - BETA_ONE**STEP)
    second_hat = second_new / (1.0 - BETA_TWO**STEP)
    param_new = param - LEARN_RATE * (
        moment_hat / (jnp.sqrt(second_hat) + EPSILON) + WEIGHT_DECAY * param
    )
    return (param_new, moment_new, second_new)


def place_kernel(pieces, skip, *refs):
    count = 1 + max(p[0] for p in pieces)
    arrays, refs = refs[:count], refs[count + skip :]
    keys_ref, values_ref, sems = refs
    half = keys_ref.shape[1]
    starts = block_rows(keys_ref.shape[0] // 8, False)
    stores = []
    for n, (array, src, size, block, low) in enumerate(pieces):
        to = pl.multiple_of(starts[block] + low, size)
        for side, out in enumerate((keys_ref, values_ref)):
            store = pltpu.make_async_copy(
                arrays[array].at[pl.ds(src, size), pl.ds(side * half, half)],
                out.at[pl.ds(to, size), :],
                sems.at[2 * n + side],
            )
            store.start()
            stores.append(store)
    for store in stores:
        store.wait()


def place(arrays, pieces, keys, started=()):
    wide = arrays[0].shape[1]
    out = jax.ShapeDtypeStruct((keys, wide // 2), BF16)
    anywhere = pl.BlockSpec(memory_space=pltpu.HBM)
    first = len(arrays)
    return pl.pallas_call(
        functools.partial(place_kernel, pieces, len(started)),
        out_shape=[out, out],
        in_specs=[pl.BlockSpec(memory_space=pltpu.VMEM)] * first + [anywhere] * len(started),
        out_specs=[anywhere] * 2,
        input_output_aliases={first + i: i for i in range(len(started))},
        scratch_shapes=[pltpu.SemaphoreType.DMA((2 * len(pieces),))],
        compiler_params=pltpu.CompilerParams(vmem_limit_bytes=16 << 20),
        name="place",
    )(*arrays, *started)


def pack_kernel(keys_ref, values_ref, out_ref):
    both = jnp.concatenate([keys_ref[...], values_ref[...]], axis=1).astype(BF16)
    out_ref[...] = jnp.broadcast_to(both, out_ref.shape)


def pack(head, keys, values, copies=()):
    share = keys.shape[0]
    shape = (*copies, share, 2 * HEAD)
    half = pl.BlockSpec((share, HEAD), lambda i: (0, head))
    return pl.pallas_call(
        pack_kernel,
        grid=(1,),
        out_shape=jax.ShapeDtypeStruct(shape, BF16),
        in_specs=[half, half],
        out_specs=pl.BlockSpec(shape, lambda i: (0,) * len(shape)),
        cost_estimate=pl.CostEstimate(flops=0, bytes_accessed=1 << 20, transcendentals=0),
        name="pack",
    )(keys, values)


def update_kernel(serve, *refs):
    grads, olds, outs = refs[:4], refs[4:10], refs[10:]
    size = grads[0].shape[0]
    turns = quarter_rows(size)
    for j in range(4):
        at = pl.ds(pl.multiple_of(turns[j], size), size)
        for head in range(2):
            cols = slice(head * HEAD, (head + 1) * HEAD)
            for side in range(2):
                low = (2 * head + side) * HEAD
                grad = grads[j][:, low : low + HEAD].astype(F32)
                new = adamw_step(*[olds[2 * n + side][at, cols] for n in range(3)], grad)
                if serve:
                    low = (2 * side + head) * HEAD
                    outs[0][at, low : low + HEAD] = new[0].astype(BF16)
                else:
                    for n in range(3):
                        outs[2 * n + side][at, cols] = new[n]
                    outs[6 + side][at, cols] = grad


def update(serve, grads, olds):
    share, half = olds[0].shape
    vm = pl.BlockSpec(memory_space=pltpu.VMEM)
    shard = jax.ShapeDtypeStruct((share, half), F32)
    served = jax.ShapeDtypeStruct((share, 2 * half), BF16)
    outs = [served] if serve else [shard] * 8
    return pl.pallas_call(
        functools.partial(update_kernel, serve),
        out_shape=outs,
        in_specs=[vm] * 10,
        out_specs=[vm] * len(outs),
        cost_estimate=pl.CostEstimate(flops=0, bytes_accessed=8 << 20, transcendentals=0),
        compiler_params=pltpu.CompilerParams(vmem_limit_bytes=24 << 20),
        name="serve" if serve else "update",
    )(*grads, *olds)


def per_device(
    queries,
    d_out,
    conv_keys,
    conv_values,
    segment_ids,
    master_keys,
    master_values,
    moment_keys,
    moment_values,
    second_keys,
    second_values,
):
    share = master_keys.shape[0]
    relayed = relay_pieces(share)

    def attention(group, arrays, pieces):
        tokens = (segment_ids, queries, d_out, conv_keys, conv_values)
        return attend(group, group == 0, *tokens, arrays, pieces)

    later = pack(1, master_keys, master_values, (8,))
    first = relay_gather(pack(0, master_keys, master_values))
    *early, later = lax.optimization_barrier((*first[:7], later))
    first = (*early, *first[7:])
    (both_part,) = attention(0, first, relayed)
    second = lax.all_to_all(later, "dp", 0, 0, tiled=True).reshape(8 * share, 2 * HEAD)
    keys_part, *values_part = attention(1, [second], [(0, b * share, share, b, 0) for b in range(8)])
    first_sum = dp_sum(both_part).astype(BF16)
    keys_sum = dp_sum(keys_part)
    values_sum = replica_sum(values_part).astype(BF16)
    low = jnp.concatenate([first_sum, keys_sum.astype(BF16)], axis=2)
    most = replica_sum([low[j] for j in range(4)])
    rest = lines_sum(values_sum)
    both = jnp.concatenate([most, rest], axis=1).astype(BF16)
    grads = [both] + [turn(both, -j) for j in (1, 2, 3)]
    olds = (master_keys, master_values, moment_keys, moment_values, second_keys, second_values)
    (served,) = update(True, grads, olds)
    *news, grad_keys, grad_values = update(False, grads, olds)
    arrays = relay_gather(served)
    started = ()
    for low, high in ((0, 4), (4, 7), (7, 9)):
        part = [(p[0] - low, *p[1:]) for p in relayed if low <= p[0] < high]
        started = place(arrays[low:high], part, 8 * share, started)
    return (*news, *started, grad_keys, grad_values)


def solution(mesh):
    tokens = P(("dp", "replica"), "tensor")
    shard = P("dp", "tensor")
    served = P(None, "tensor")
    return jax.shard_map(
        per_device,
        mesh=mesh,
        in_specs=(tokens,) * 4 + (P(("dp", "replica"), None),) + (shard,) * 6,
        out_specs=(shard,) * 6 + (served,) * 2 + (shard,) * 2,
        check_vma=False,
    )
```
